256 devices in a mesh: branch: 32 (over z, y_lo, core), bus: 8 (over x, y_hi).
Axes of the slice: x: 4, y: 4 (y_hi: 2, y_lo: 2; y = y_hi * 2 + y_lo), z: 8, core: 2. Of those that a mesh axis runs over, the one named last changes fastest.
Arguments:
- injections: float32 [512, 60416], P('branch', 'bus'), may hold values from -0.0234375 to 0.0234375
- ptdf_mon: float32 [4096, 60416], P('branch', 'bus'), may hold values from -2.5 to 2.5
- ptdf_out: float32 [2048, 60416], P('branch', 'bus'), may hold values from -2.5 to 2.5
- outage_from: int32 [2048], replicated, may hold values from 0 to 60415
- outage_to: int32 [2048], replicated, may hold values from 0 to 60415
- hour_ids: int32 [512], P('bus'), may hold values from 0 to 8759
- ratings: float32 [4096, 4], P('branch'), may hold values from 0.5 to 2
Outputs:
- worst_loading: float32 [512, 4096], P('bus', 'branch')
The draws below stay inside these ranges and needn't reach their ends.
All inputs are finite; a program needn't handle non-finite values.
Results may differ from the reference program's by a relative error of at most 0.00019.
Values sent between devices are 32-bit elements; how exact they have to be, the bound alone decides.
A program may use at most 128 MiB of HBM per device.

```python
import math
import jax
import jax.numpy as jnp
from jax import lax

NB = 60416
HOURS = 512
SEASONS = 4
MONITORED = 4096
OUTAGES = 2048


def touch_ends(values, rng, smallest, high):
    dims = values.shape
    place = [jax.random.randint(jax.random.fold_in(rng, axis), (), 0, dims[axis]) for axis in range(len(dims))]
    values = values.at[tuple(place)].set(smallest)
    longest = dims.index(max(dims))
    place[longest] = (place[longest] + 1) % dims[longest]
    return values.at[tuple(place)].set(high)


def steps_of(rng, shape, pieces, smallest, top_value):
    factor_of = 1.0
    for position, shards_of in pieces:
        heights = jax.random.uniform(jax.random.fold_in(jax.random.fold_in(rng, 6), position), (shards_of,), jnp.float32, smallest / len(pieces), top_value / len(pieces))
        factor_of = factor_of * jnp.repeat(jnp.exp(heights), shape[position] // shards_of).reshape((-1,) + (1,) * (len(shape) - 1 - position))
    return factor_of


def centred(rng, dims, width, most, split=(), held_as=jnp.bfloat16):
    loudness = steps_of(rng, dims, split, -0.22, 0.18) if split else 1.0
    drawn = jax.random.normal(rng, dims, jnp.float32) * width * loudness
    return jnp.minimum(jnp.maximum(drawn, -most), most).astype(held_as)


def setup_inputs(seed: int = 0) -> dict:
    arg_keys = jax.random.split(jax.random.key(seed), 8)
    injections = centred(arg_keys[0], (HOURS, NB), NB ** -0.5, 0.0234375, ((0, 32), (1, 8)), jnp.float32)
    ptdf_mon = centred(arg_keys[1], (MONITORED, NB), 0.35, 2.5, ((0, 32), (1, 8)), jnp.float32)
    ptdf_out = centred(arg_keys[2], (OUTAGES, NB), 0.35, 2.5, ((0, 32), (1, 8)), jnp.float32)
    outage_from = touch_ends(jax.random.randint(arg_keys[3], (OUTAGES,), 0, NB), jax.random.fold_in(arg_keys[3], 1), 0, NB - 1).astype(jnp.int32)
    outage_to = touch_ends(jax.random.randint(arg_keys[4], (OUTAGES,), 0, NB), jax.random.fold_in(arg_keys[4], 1), 0, NB - 1).astype(jnp.int32)
    hour_ids = touch_ends(jax.random.randint(arg_keys[5], (HOURS,), 0, 8760), jax.random.fold_in(arg_keys[5], 1), 0, 8759).astype(jnp.int32)
    ratings = jnp.clip(jnp.exp(math.log(2.0) - 1.3862944 * jax.random.uniform(arg_keys[6], (MONITORED, SEASONS), jnp.float32) ** steps_of(arg_keys[6], (MONITORED, SEASONS), ((0, 32),), -0.2, 0.2)), 0.5, 2.0)
    return dict(injections=injections, ptdf_mon=ptdf_mon, ptdf_out=ptdf_out, outage_from=outage_from, outage_to=outage_to, hour_ids=hour_ids, ratings=ratings)


def reference(injections, ptdf_mon, ptdf_out, outage_from, outage_to, hour_ids, ratings):
    highest = lax.Precision.HIGHEST
    base_mon = jnp.dot(injections, ptdf_mon.T, precision=highest, preferred_element_type=jnp.float32)
    base_out = jnp.dot(injections, ptdf_out.T, precision=highest, preferred_element_type=jnp.float32)
    sens = jnp.take(ptdf_mon, outage_from, axis=1) - jnp.take(ptdf_mon, outage_to, axis=1)
    rows_index = jnp.arange(OUTAGES, dtype=jnp.int32)
    self_sens = ptdf_out[rows_index, outage_from] - ptdf_out[rows_index, outage_to]
    lodf_t = (sens / jnp.maximum(1.0 - self_sens, 0.25)[None, :]).T
    block_size = 32
    def advance(index, worst_load):
        first = (index * block_size).astype(jnp.int32)
        lodf_block = lax.dynamic_slice_in_dim(lodf_t, first, block_size, 0)
        flow_block = lax.dynamic_slice_in_dim(base_out, first, block_size, 1)
        after_outage = base_mon[:, None, :] + flow_block[:, :, None] * lodf_block[None, :, :]
        return jnp.maximum(worst_load, jnp.max(jnp.abs(after_outage), axis=1))
    worst_load = lax.fori_loop(0, OUTAGES // block_size, advance, jnp.abs(base_mon))
    season = (hour_ids * 4) // 8760
    onehot = (season[:, None] == jnp.arange(SEASONS, dtype=jnp.int32)[None, :]).astype(jnp.float32)
    hour_rating = jnp.dot(onehot, ratings.T, precision=highest, preferred_element_type=jnp.float32)
    return worst_load / hour_rating
```

```python
import functools

import jax
import jax.numpy as jnp
from jax import lax
from jax.experimental import pallas as pl
from jax.experimental.pallas import tpu as pltpu
from jax.sharding import PartitionSpec as P

MESH = pl.DeviceIdType.MESH
F32 = jnp.float32
BF16 = jnp.bfloat16
NT = (((1,), (1,)), ((), ()))


def split_bf16(x):
    hi = x.astype(BF16)
    return hi, (x - hi.astype(F32)).astype(BF16)


def gather_kernel(
    inj, mon, out, ids_from, ids_to,
    flows, sens, self_out,
    a, b32, bhi, blo, frm, too, onehot,
    zs, zr, ys, yr, cs, cr, bsem,
):
    me = lax.axis_index("branch")
    bus = lax.axis_index("bus")
    width = mon.shape[1]
    mrows, orows = mon.shape[0], out.shape[0]
    z = me // 4
    y = (me // 2) % 2
    p = me % 2
    oy = 1 - y
    up = {"branch": (me + 4) % 32}
    down = {"branch": (me + 28) % 32}
    across = {"branch": z * 4 + oy * 2 + p}
    mate = {"branch": z * 4 + y * 2 + (1 - p)}

    load_b = [
        pltpu.make_async_copy(mon, b32.at[pl.ds(0, mrows)], bsem.at[0]),
        pltpu.make_async_copy(out, b32.at[pl.ds(mrows, orows)], bsem.at[1]),
    ]
    own_copy = [
        pltpu.make_async_copy(inj.at[pl.ds(8 * e, 8)], a.at[z, y, p, e], bsem.at[2 + e])
        for e in range(2)
    ]
    for c in load_b + own_copy:
        c.start()

    barrier = pltpu.get_barrier_semaphore()
    for d in (up, down, across, mate):
        pl.semaphore_signal(barrier, inc=1, device_id=d, device_id_type=MESH)
    pl.semaphore_wait(barrier, 4)

    def slot(delta):
        return (z + (delta + 8)) % 8

    def chunk(delta, yy, pp, e):
        return a.at[slot(delta), yy, pp, e]

    sends = []

    def send(src, dst, ssem, rsem, dev):
        c = pltpu.make_async_remote_copy(
            src_ref=src, dst_ref=dst, send_sem=ssem, recv_sem=rsem,
            device_id=dev, device_id_type=MESH,
        )
        c.start()
        sends.append(c)

    def arrived(ref, rsem):
        pltpu.make_async_remote_copy(
            src_ref=ref, dst_ref=ref, send_sem=rsem, recv_sem=rsem,
            device_id=mate, device_id_type=MESH,
        ).wait_recv()

    def send_z(direction, item):
        sign = 1 if direction == 0 else -1
        if item < 6:
            step, e, yy = item // 2 + 1, item % 2, y
        elif item == 6:
            step, e, yy = 4, direction, y
        else:
            step, e, yy = item - 6, 0, oy
        delta = -sign * (step - 1)
        dst = chunk(delta, yy, p, e)
        src = inj.at[pl.ds(8 * e, 8)] if item < 2 else dst
        send(src, dst, zs.at[direction, item], zr.at[direction, item], up if direction == 0 else down)

    def recv_z(direction, item):
        sign = 1 if direction == 0 else -1
        if item < 6:
            step, e, yy = item // 2 + 1, item % 2, y
        elif item == 6:
            step, e, yy = 4, direction, y
        else:
            step, e, yy = item - 6, 0, oy
        delta = -sign * step
        arrived(chunk(delta, yy, p, e), zr.at[direction, item])
        send_c(delta, yy, e)

    y_items = [(0, 0), (0, 1), (-1, 1), (1, 1), (-2, 1), (2, 1), (-3, 1), (3, 1), (-4, 0), (-4, 1)]

    def send_y(item):
        delta, e = y_items[item]
        dst = chunk(delta, y, p, e)
        src = inj.at[pl.ds(8 * e, 8)] if item < 2 else dst
        send(src, dst, ys.at[item], yr.at[item], across)

    def recv_y(item):
        delta, e = y_items[item]
        arrived(chunk(delta, oy, p, e), yr.at[item])
        send_c(delta, oy, e)

    c_items = []

    def send_c(delta, yy, e):
        item = len(c_items)
        other = 0 if yy is y else 1
        c_items.append((delta, other, e))
        dst = chunk(delta, yy, p, e)
        src = inj.at[pl.ds(8 * e, 8)] if (delta == 0 and other == 0) else dst
        send(src, dst, cs.at[item], cr.at[item], mate)

    got_c = set()

    def recv_c(deltas):
        for item, (delta, other, e) in enumerate(c_items):
            if delta in deltas and item not in got_c:
                got_c.add(item)
                arrived(chunk(delta, oy if other else y, 1 - p, e), cr.at[item])

    def block(delta):
        k = slot(delta)
        x = a[k].reshape(64, width)
        hi, lo = split_bf16(x)
        acc = lax.dot_general(hi, bhi[...], NT, preferred_element_type=F32)
        acc = acc + lax.dot_general(lo, bhi[...], NT, preferred_element_type=F32)
        acc = acc + lax.dot_general(hi, blo[...], NT, preferred_element_type=F32)
        flows[pl.ds(pl.multiple_of(k * 64, 64), 64)] = acc

    shift = bus * width

    def index_columns():
        f = ids_from[...] - shift
        t = ids_to[...] - shift
        same = f == t
        f = jnp.where(same, -1, f)
        t = jnp.where(same, -1, t)
        for i in range(f.shape[0]):
            frm[pl.ds(i * 128, 128)] = jnp.broadcast_to(f[i:i + 1], (128, 128)).T
            too[pl.ds(i * 128, 128)] = jnp.broadcast_to(t[i:i + 1], (128, 128)).T

    tiles = width // 128
    lane = lax.broadcasted_iota(jnp.int32, (1, 128), 1)

    def self_part():
        rows = pl.ds(pl.multiple_of(me * orows, orows), orows)
        f, t = frm[rows], too[rows]

        def step(j, acc):
            cols = pl.ds(pl.multiple_of(j * 128, 128), 128)
            v = b32[pl.ds(mrows, orows), cols]
            at = lane + j * 128
            return acc + jnp.where(f == at, v, 0.0) - jnp.where(t == at, v, 0.0)

        acc = lax.fori_loop(0, tiles, step, jnp.zeros((orows, 128), F32))
        self_out[...] = jnp.broadcast_to(jnp.sum(acc, axis=1, keepdims=True), (orows, 128))

    def sens_part(n):
        size = 256
        rows = pl.ds(n * size, size)

        def step(j, _):
            cols = pl.ds(pl.multiple_of(j * 128, 128), 128)
            at = lane + j * 128
            onehot[:, cols] = jnp.where(
                frm[rows] == at, 1.0, jnp.where(too[rows] == at, -1.0, 0.0)
            ).astype(BF16)
            return 0

        lax.fori_loop(0, tiles, step, 0)
        acc = lax.dot_general(bhi[pl.ds(0, mrows)], onehot[...], NT, preferred_element_type=F32)
        acc = acc + lax.dot_general(blo[pl.ds(0, mrows)], onehot[...], NT, preferred_element_type=F32)
        sens[:, rows] = acc

    for e in range(2):
        send_z(0, e)
        send_z(1, e)
        send_y(e)
        send_c(0, y, e)
    for c in load_b:
        c.wait()
    index_columns()
    for r in range(0, mrows + orows, 64):
        hi, lo = split_bf16(b32[pl.ds(r, 64)])
        bhi[pl.ds(r, 64)] = hi
        blo[pl.ds(r, 64)] = lo
    for c in own_copy:
        c.wait()

    both = (0, 1)
    for d in both:
        recv_z(d, 0)
        send_z(d, 2)
    recv_y(0)
    self_part()
    for d in both:
        recv_z(d, 1)
        send_z(d, 3)
    send_y(2), send_y(3)
    recv_y(1)
    for d in both:
        send_z(d, 7)
    sens_part(0)
    for d in both:
        recv_z(d, 2)
        send_z(d, 4)
    sens_part(1)
    for d in both:
        recv_z(d, 3)
        send_z(d, 5)
    send_y(4), send_y(5)
    recv_y(2), recv_y(3)
    for d in both:
        recv_z(d, 7)
        send_z(d, 8)
    sens_part(2)
    recv_z(0, 4)
    send_z(0, 6)
    recv_z(1, 4)
    sens_part(3)
    recv_z(0, 5)
    recv_z(1, 5)
    send_z(1, 6)
    send_y(6), send_y(7)
    recv_y(4), recv_y(5)
    for d in both:
        recv_z(d, 8)
        send_z(d, 9)
    for n in range(4, 8):
        sens_part(n)
    recv_c((0, 1, -1))
    recv_z(0, 6)
    send_y(8)
    recv_z(1, 6)
    send_y(9)
    block(0)
    block(1)
    block(-1)
    recv_y(6), recv_y(7)
    recv_c((2, -2))
    block(2)
    block(-2)
    for d in both:
        recv_z(d, 9)
    recv_y(8), recv_y(9)
    recv_c((3, -3, 4, -4))
    block(3)
    block(-3)
    block(-4)
    for c in sends:
        c.wait_send()


def gather_flows(injections, ptdf_mon, ptdf_out, outage_from, outage_to):
    mrows, width = ptdf_mon.shape
    orows = ptdf_out.shape[0]
    outages = outage_from.shape[0]
    hours = injections.shape[0] * lax.axis_size("branch")
    rows = mrows + orows
    hbm = pl.BlockSpec(memory_space=pl.ANY)
    vmem = pl.BlockSpec(memory_space=pltpu.VMEM)
    dma = pltpu.SemaphoreType.DMA
    return pl.pallas_call(
        gather_kernel,
        out_shape=(
            jax.ShapeDtypeStruct((hours, rows), F32),
            jax.ShapeDtypeStruct((mrows, outages), F32),
            jax.ShapeDtypeStruct((orows, 128), F32),
        ),
        in_specs=[hbm, hbm, hbm, vmem, vmem],
        out_specs=(vmem, vmem, vmem),
        scratch_shapes=[
            pltpu.VMEM((8, 2, 2, 2, 8, width), F32),
            pltpu.VMEM((rows, width), F32),
            pltpu.VMEM((rows, width), BF16),
            pltpu.VMEM((rows, width), BF16),
            pltpu.VMEM((outages, 128), jnp.int32),
            pltpu.VMEM((outages, 128), jnp.int32),
            pltpu.VMEM((256, width), BF16),
            dma((2, 10)), dma((2, 10)), dma((10,)), dma((10,)), dma((32,)), dma((32,)), dma((4,)),
        ],
        compiler_params=pltpu.CompilerParams(
            collective_id=0, has_side_effects=True, vmem_limit_bytes=64 * 1024 * 1024 - 128 * 1024
        ),
        name="gather_flows",
    )(injections, ptdf_mon, ptdf_out, outage_from.reshape(-1, 128), outage_to.reshape(-1, 128))


def screen(base_mon, outage_base, lodf_t, block_size):
    outage_count = lodf_t.shape[0]

    def advance(index, worst_load):
        first = index * block_size
        lodf_block = lax.dynamic_slice_in_dim(lodf_t, first, block_size, 0)
        flow_block = lax.dynamic_slice_in_dim(outage_base, first, block_size, 1)
        after_outage = base_mon[:, None, :] + flow_block[:, :, None] * lodf_block[None, :, :]
        return jnp.maximum(worst_load, jnp.max(jnp.abs(after_outage), axis=1))

    return lax.fori_loop(0, outage_count // block_size, advance, jnp.abs(base_mon))


def on_device(injections, ptdf_mon, ptdf_out, outage_from, outage_to, hour_ids, ratings):
    highest = lax.Precision.HIGHEST
    mon_rows = ptdf_mon.shape[0]
    bus_count = lax.axis_size("bus")
    bus_index = lax.axis_index("bus")
    partial_flows, sens_part, self_part = gather_flows(
        injections, ptdf_mon, ptdf_out, outage_from, outage_to
    )
    hours_dev = partial_flows.shape[0] // bus_count
    summed_flows, sens_mon, self_sens = lax.psum((partial_flows, sens_part, self_part[:, 0]), "bus")
    base_flows = lax.dynamic_slice_in_dim(summed_flows, bus_index * hours_dev, hours_dev, 0)
    base_mon = base_flows[:, :mon_rows]
    base_out = base_flows[:, mon_rows:]
    outage_base, outage_self = (
        lax.all_gather(base_out, "branch", axis=1, tiled=True),
        lax.all_gather(self_sens, "branch", axis=0, tiled=True),
    )
    divisor = jnp.maximum(1.0 - outage_self, 0.25)
    lodf_t = (sens_mon / divisor[None, :]).T
    worst_load = screen(base_mon, outage_base, lodf_t, min(256, lodf_t.shape[0]))
    season = hour_ids * 4 // 8760
    onehot = (season[:, None] == jnp.arange(ratings.shape[1], dtype=jnp.int32)[None, :]).astype(
        jnp.float32
    )
    hour_rating = jnp.dot(onehot, ratings.T, precision=highest, preferred_element_type=jnp.float32)
    return worst_load / hour_rating


def solution(mesh):
    placed = (
        P("branch", "bus"),
        P("branch", "bus"),
        P("branch", "bus"),
        P(),
        P(),
        P("bus"),
        P("branch", None),
    )
    return jax.shard_map(
        on_device, mesh=mesh, in_specs=placed, out_specs=P("bus", "branch"), check_vma=False
    )
```

```python
import functools

import jax
import jax.numpy as jnp
from jax import lax
from jax.experimental import pallas as pl
from jax.experimental.pallas import tpu as pltpu
from jax.sharding import PartitionSpec as P

MESH = pl.DeviceIdType.MESH
F32 = jnp.float32
BF16 = jnp.bfloat16
NT = (((1,), (1,)), ((), ()))


def split_bf16(x):
    hi = x.astype(BF16)
    return hi, (x - hi.astype(F32)).astype(BF16)


def screen_kernel(
    inj, mon, out, ids_from, ids_to, hour_ids, ratings,
    result,
    a, b32, bl, bthi, btlo, onehot, ahi, alo,
    part, parts3, tot, qsum, lod, send_flow, recv_flow, packs, fscr,
    zs, zr, ys, yr, cs, cr, bsem, xs, xr, fs, fr, pzs, pzr, pys, pyr, pcs, pcr,
):
    me = lax.axis_index("branch")
    bus = lax.axis_index("bus")
    width = mon.shape[1]
    mrows, orows = mon.shape[0], out.shape[0]
    z = me // 4
    y = (me // 2) % 2
    p = me % 2
    oy = 1 - y
    x = bus // 2
    h = bus % 2
    up = {"branch": (me + 4) % 32}
    down = {"branch": (me + 28) % 32}
    across = {"branch": z * 4 + oy * 2 + p}
    mate = {"branch": z * 4 + y * 2 + (1 - p)}

    load_b = [
        pltpu.make_async_copy(mon, b32.at[pl.ds(0, mrows)], bsem.at[0]),
        pltpu.make_async_copy(out, b32.at[pl.ds(mrows, orows)], bsem.at[1]),
    ]
    own_copy = [
        pltpu.make_async_copy(inj.at[pl.ds(8 * e, 8)], a.at[z, y, p, e], bsem.at[2 + e])
        for e in range(2)
    ]
    for c in load_b + own_copy:
        c.start()

    barrier = pltpu.get_barrier_semaphore()
    peers = [across, mate]
    peers += [{"branch": (me + 4 * k) % 32} for k in range(1, 8)]
    peers += [{"bus": (bus + k) % 8} for k in range(1, 8)]
    for d in peers:
        pl.semaphore_signal(barrier, inc=1, device_id=d, device_id_type=MESH)
    pl.semaphore_wait(barrier, len(peers))

    def slot(delta):
        return (z + (delta + 8)) % 8

    def chunk(delta, yy, pp, e):
        return a.at[slot(delta), yy, pp, e]

    sends = []

    def send(src, dst, ssem, rsem, dev):
        c = pltpu.make_async_remote_copy(
            src_ref=src, dst_ref=dst, send_sem=ssem, recv_sem=rsem,
            device_id=dev, device_id_type=MESH,
        )
        c.start()
        sends.append(c)

    def arrived(ref, rsem):
        pltpu.make_async_remote_copy(
            src_ref=ref, dst_ref=ref, send_sem=rsem, recv_sem=rsem,
            device_id=mate, device_id_type=MESH,
        ).wait_recv()

    def z_item(direction, item):
        if item < 6:
            return item // 2 + 1, item % 2, y
        if item == 6:
            return 4, direction, y
        return item - 6, 0, oy

    def send_z(direction, item):
        sign = 1 if direction == 0 else -1
        step, e, yy = z_item(direction, item)
        dst = chunk(-sign * (step - 1), yy, p, e)
        src = inj.at[pl.ds(8 * e, 8)] if item < 2 else dst
        send(src, dst, zs.at[direction, item], zr.at[direction, item], up if direction == 0 else down)

    def recv_z(direction, item):
        sign = 1 if direction == 0 else -1
        step, e, yy = z_item(direction, item)
        delta = -sign * step
        arrived(chunk(delta, yy, p, e), zr.at[direction, item])
        return lambda: send_c(delta, yy, e)

    y_items = [(0, 0), (0, 1), (-1, 1), (1, 1), (-2, 1), (2, 1), (-3, 1), (3, 1), (-4, 0), (-4, 1)]

    def send_y(item):
        delta, e = y_items[item]
        dst = chunk(delta, y, p, e)
        src = inj.at[pl.ds(8 * e, 8)] if item < 2 else dst
        send(src, dst, ys.at[item], yr.at[item], across)

    def recv_y(item):
        delta, e = y_items[item]
        arrived(chunk(delta, oy, p, e), yr.at[item])
        return lambda: send_c(delta, oy, e)

    c_items = []

    def send_c(delta, yy, e):
        item = len(c_items)
        other = 0 if yy is y else 1
        c_items.append((delta, other, e))
        dst = chunk(delta, yy, p, e)
        src = inj.at[pl.ds(8 * e, 8)] if (delta == 0 and other == 0) else dst
        send(src, dst, cs.at[item], cr.at[item], mate)

    got_c = set()

    def recv_c(deltas):
        for item, (delta, other, e) in enumerate(c_items):
            if delta in deltas and item not in got_c:
                got_c.add(item)
                arrived(chunk(delta, oy if other else y, 1 - p, e), cr.at[item])

    tiles = width // 128

    def block(deltas):
        rows = 64 * len(deltas)
        for n, delta in enumerate(deltas):
            hi, lo = split_bf16(a[slot(delta)].reshape(64, width))
            ahi[pl.ds(64 * n, 64)] = hi
            alo[pl.ds(64 * n, 64)] = lo
        top = pl.ds(0, rows)
        acc = jnp.dot(ahi[top], bthi[...], preferred_element_type=F32)
        acc = acc + jnp.dot(alo[top], bthi[...], preferred_element_type=F32)
        acc = acc + jnp.dot(ahi[top], btlo[...], preferred_element_type=F32)
        for n, delta in enumerate(deltas):
            k = slot(delta)
            got = acc[64 * n:64 * n + 64]
            send_flow[k, pl.ds(0, 64)] = got[:, :mrows]
            tail = got[:, mrows:]
            send_flow[k, pl.ds(64, 32)] = jnp.concatenate([tail[:32], tail[32:]], axis=1)

    shift = bus * width

    def transposed_b():
        def step(j, _):
            cols = pl.ds(pl.multiple_of(j * 128, 128), 128)
            for r, n in ((0, mrows), (mrows, orows)):
                hi, lo = split_bf16(b32[pl.ds(r, n), cols].T)
                bthi[cols, pl.ds(r, n)] = hi
                btlo[cols, pl.ds(r, n)] = lo
            return 0

        lax.fori_loop(0, tiles, step, 0)

    def left_b():
        for r in range(0, mrows, 32):
            hi, lo = split_bf16(b32[pl.ds(r, 32)])
            bl[pl.ds(r, 32)] = hi
            bl[pl.ds(mrows + r, 32)] = lo

    def index_rows(start, size):
        cols = pl.ds(pl.multiple_of(start, 128), size)
        f = ids_from[:, cols] - shift
        t = ids_to[:, cols] - shift
        same = f == t
        return jnp.where(same, -1, f), jnp.where(same, -1, t)

    def self_part():
        chip = me // 2
        f, t = index_rows(chip * 128, 128)
        f = jnp.broadcast_to(f, (128, 128)).T
        t = jnp.broadcast_to(t, (128, 128)).T
        mine = p == 0
        f = jnp.where(mine, f[:orows], f[orows:])
        t = jnp.where(mine, t[:orows], t[orows:])
        lane = lax.broadcasted_iota(jnp.int32, (1, 128), 1)

        def step(j, acc):
            cols = pl.ds(pl.multiple_of(j * 128, 128), 128)
            v = b32[pl.ds(mrows, orows), cols]
            at = lane + j * 128
            return acc + jnp.where(f == at, v, 0.0) - jnp.where(t == at, v, 0.0)

        acc = lax.fori_loop(0, tiles, step, jnp.zeros((orows, 128), F32))
        acc = jnp.concatenate([acc, jnp.zeros((128 - orows, 128), F32)], axis=0)
        row = jnp.sum(acc.T, axis=0, keepdims=True)
        for k in range(8):
            send_flow[k, pl.ds(96, 8)] = jnp.broadcast_to(row, (8, 128))

    def sens_part(d, half):
        i = (x + d) % 4
        f, t = index_rows(i * 512 + half * 256, 256)
        sub = lax.broadcasted_iota(jnp.int32, (128, 256), 0)

        def step(j, _):
            at = sub + j * 128
            onehot[pl.ds(pl.multiple_of(j * 128, 128), 128)] = jnp.where(
                f == at, 1.0, jnp.where(t == at, -1.0, 0.0)
            ).astype(BF16)
            return 0

        lax.fori_loop(0, tiles, step, 0)
        acc = jnp.dot(bl[...], onehot[...], preferred_element_type=F32)
        part[i, :, pl.ds(half * 256, 256)] = acc[:mrows] + acc[mrows:]

    def x_dev(d):
        return {"bus": ((x + d) % 4) * 2 + h}

    def send_part(d):
        send(part.at[(x + d) % 4], parts3.at[d - 1], xs.at[d - 1], xr.at[d - 1], x_dev(d))

    def sum_part():
        for d in (1, 2, 3):
            arrived(parts3.at[d - 1], xr.at[d - 1])
        tot[...] = part[x] + parts3[0] + parts3[1] + parts3[2]
        send(tot, qsum, xs.at[3], xr.at[3], {"bus": x * 2 + (1 - h)})

    def share_part():
        arrived(qsum, xr.at[3])
        sends[pair_send[0]].wait_send()
        lod[x] = tot[...] + qsum[...]
        for d in (1, 2, 3):
            send(lod.at[x], lod.at[x], xs.at[3 + d], xr.at[3 + d], x_dev(d))

    def take_part():
        for d in (1, 2, 3):
            arrived(lod.at[(x + 4 - d) % 4], xr.at[3 + d])

    pair_send = []

    def both(f, *items):
        for item in items:
            for d in (0, 1):
                f(d, item)

    def recv_both(item):
        return [recv_z(0, item), recv_z(1, item)]

    def run(fs_):
        for f_ in fs_:
            f_()

    for e in range(2):
        send_z(0, e)
        send_z(1, e)
        send_y(e)
        send_c(0, y, e)
    for c in load_b:
        c.wait()
    left_b()
    for c in own_copy:
        c.wait()
    sens_part(2, 0)
    q = recv_both(0)
    both(send_z, 2)
    q += [recv_y(0)]
    run(q)
    sens_part(2, 1)
    send_part(2)
    q = recv_both(1)
    both(send_z, 3)
    send_y(2), send_y(3)
    q += [recv_y(1)]
    both(send_z, 7)
    run(q)
    sens_part(1, 0)
    sens_part(1, 1)
    send_part(1)
    q = recv_both(2)
    both(send_z, 4)
    run(q)
    sens_part(3, 0)
    sens_part(3, 1)
    send_part(3)
    q = recv_both(3)
    both(send_z, 5)
    send_y(4), send_y(5)
    q += [recv_y(2), recv_y(3)]
    run(q)
    sens_part(0, 0)
    q = recv_both(7)
    both(send_z, 8)
    run(q)
    sens_part(0, 1)
    sum_part()
    pair_send.append(len(sends) - 1)
    q = [recv_z(0, 4)]
    send_z(0, 6)
    q += [recv_z(1, 4)]
    run(q)
    self_part()
    transposed_b()
    share_part()
    q = recv_both(5)
    send_z(1, 6)
    send_y(6), send_y(7)
    q += [recv_y(4), recv_y(5)]
    run(q)
    q = recv_both(8)
    both(send_z, 9)
    run(q)
    recv_c((0, 1, -1))
    block((0,))
    q = [recv_z(0, 6)]
    send_y(8)
    q += [recv_z(1, 6)]
    send_y(9)
    run(q)
    block((1, -1))
    run([recv_y(6), recv_y(7)])
    recv_c((2, -2))
    block((2, -2))
    run(recv_both(9) + [recv_y(8), recv_y(9)])
    recv_c((3, -3, 4, -4))
    block((3, -3, -4))

    for k in range(1, 8):
        to = (bus + k) % 8
        send(send_flow.at[to], recv_flow.at[k], fs.at[k], fr.at[k], {"bus": to})
    own = send_flow[bus]
    for k in range(1, 8):
        arrived(recv_flow.at[k], fr.at[k])
        own = own + recv_flow[k]
    recv_flow[0] = own
    packs[z, y, p] = recv_flow[0, pl.ds(64, 40)]

    def pack_to_y(k, zz):
        send(packs.at[zz, y, p], packs.at[zz, y, p], pys.at[k], pyr.at[k], across)

    def pack_to_c(k, zz, yy):
        send(packs.at[zz, yy, p], packs.at[zz, yy, p], pcs.at[k], pcr.at[k], mate)

    for k in (4, 3, 5, 2, 6, 1, 7):
        send(packs.at[z, y, p], packs.at[z, y, p], pzs.at[k], pzr.at[k], {"branch": (me + 4 * k) % 32})
    pack_to_y(0, z)
    pack_to_c(0, z, y)
    order = (1, 7, 2, 6, 3, 5, 4)
    for k in order:
        zz = (z + 8 - k) % 8
        arrived(packs.at[zz, y, p], pzr.at[k])
        pack_to_y(k, zz)
        pack_to_c(k, zz, y)
    for k in (0,) + order:
        zz = (z + 8 - k) % 8
        arrived(packs.at[zz, oy, p], pyr.at[k])
        pack_to_c(8 + k, zz, oy)
    for k in (0,) + order:
        zz = (z + 8 - k) % 8
        arrived(packs.at[zz, y, 1 - p], pcr.at[k])
        arrived(packs.at[zz, oy, 1 - p], pcr.at[8 + k])
    take_part()

    low = lax.broadcasted_iota(jnp.int32, (1, 128), 1) < 64

    def unpack(n, _):
        zz, yy = n // 2, n % 2
        p0, p1 = packs[zz, yy, 0], packs[zz, yy, 1]
        r0, r1 = pltpu.roll(p0, 64, 1), pltpu.roll(p1, 64, 1)
        first = jnp.where(low, p0, r1)
        second = jnp.where(low, r0, p1)
        scale = 1.0 / jnp.maximum(1.0 - first[32:33], 0.25)
        fscr[n, pl.ds(0, 32)] = first[:32] * scale
        fscr[n, pl.ds(32, 32)] = second[:32] * scale
        return 0

    lax.fori_loop(0, 16, unpack, 0)

    lane = lax.broadcasted_iota(jnp.int32, (1, 1, 128), 2)
    hb, mt = 4, 4

    def screen_m(g, _):
        rows = pl.ds(pl.multiple_of(g * (8 * mt), 8 * mt), 8 * mt)

        def screen_h(n, carry):
            top, bot = carry
            hi = [jnp.zeros((mt, 8, 128), F32) for _ in range(hb)]
            lo = [jnp.zeros((mt, 8, 128), F32) for _ in range(hb)]
            for kb in range(16):
                l = lod[kb // 4, rows, pl.ds((kb % 4) * 128, 128)].reshape(mt, 8, 128)
                for i in range(hb):
                    f = fscr[kb, pl.ds(n * hb + i, 8, stride=0)]
                    v = l * f[None]
                    hi[i] = jnp.maximum(hi[i], v)
                    lo[i] = jnp.minimum(lo[i], v)
            for i in range(hb):
                here = lane == n * hb + i
                top = jnp.where(here, jnp.max(hi[i], axis=2, keepdims=True), top)
                bot = jnp.where(here, jnp.min(lo[i], axis=2, keepdims=True), bot)
            return top, bot

        zero = jnp.zeros((mt, 8, 128), F32)
        top, bot = lax.fori_loop(0, 64 // hb, screen_h, (zero, zero))
        parts3[0, rows, pl.ds(0, 128)] = top.reshape(8 * mt, 128)
        parts3[1, rows, pl.ds(0, 128)] = bot.reshape(8 * mt, 128)
        return 0

    lax.fori_loop(0, mrows // (8 * mt), screen_m, 0)
    base = jnp.concatenate([recv_flow[0, pl.ds(0, 64)], jnp.zeros((64, 128), F32)], axis=0).T
    worst = jnp.maximum(
        jnp.abs(base + parts3[0, :, pl.ds(0, 128)]), jnp.abs(base + parts3[1, :, pl.ds(0, 128)])
    )
    hour = jnp.concatenate([hour_ids[...], jnp.zeros((1, 64), jnp.int32)], axis=1)
    season = (hour * 4) // 8760
    rating = jnp.where(season == 0, ratings[:, 0:1], ratings[:, 1:2])
    rating = jnp.where(season == 2, ratings[:, 2:3], rating)
    rating = jnp.where(season == 3, ratings[:, 3:4], rating)
    result[...] = (worst / rating).T[:64]
    done = set(pair_send)
    for n, c in enumerate(sends):
        if n not in done:
            c.wait_send()


def on_device(injections, ptdf_mon, ptdf_out, outage_from, outage_to, hour_ids, ratings):
    mrows, width = ptdf_mon.shape
    orows = ptdf_out.shape[0]
    rows = mrows + orows
    hbm = pl.BlockSpec(memory_space=pl.ANY)
    vmem = pl.BlockSpec(memory_space=pltpu.VMEM)
    dma = pltpu.SemaphoreType.DMA
    v = pltpu.VMEM
    return pl.pallas_call(
        screen_kernel,
        out_shape=jax.ShapeDtypeStruct((64, mrows), F32),
        in_specs=[hbm, hbm, hbm, vmem, vmem, vmem, vmem],
        out_specs=vmem,
        scratch_shapes=[
            v((8, 2, 2, 2, 8, width), F32),
            v((rows, width), F32),
            v((2 * mrows, width), BF16),
            v((width, rows), BF16),
            v((width, rows), BF16),
            v((width, 256), BF16),
            v((192, width), BF16),
            v((192, width), BF16),
            v((4, mrows, 512), F32),
            v((3, mrows, 512), F32),
            v((mrows, 512), F32),
            v((mrows, 512), F32),
            v((4, mrows, 512), F32),
            v((8, 104, 128), F32),
            v((8, 104, 128), F32),
            v((8, 2, 2, 40, 128), F32),
            v((16, 64, 128), F32),
            dma((2, 10)), dma((2, 10)), dma((10,)), dma((10,)), dma((32,)), dma((32,)), dma((4,)),
            dma((7,)), dma((7,)), dma((8,)), dma((8,)), dma((8,)), dma((8,)), dma((8,)), dma((8,)),
            dma((16,)), dma((16,)),
        ],
        compiler_params=pltpu.CompilerParams(
            collective_id=0, has_side_effects=True, vmem_limit_bytes=64 * 1024 * 1024 - 128 * 1024
        ),
        name="screen",
    )(
        injections, ptdf_mon, ptdf_out, outage_from.reshape(1, -1), outage_to.reshape(1, -1),
        hour_ids.reshape(1, -1), ratings,
    )


def solution(mesh):
    placed = (
        P("branch", "bus"),
        P("branch", "bus"),
        P("branch", "bus"),
        P(),
        P(),
        P("bus"),
        P("branch", None),
    )
    return jax.shard_map(
        on_device, mesh=mesh, in_specs=placed, out_specs=P("bus", "branch"), check_vma=False
    )
```

```python
import functools

import jax
import jax.numpy as jnp
from jax import lax
from jax.experimental import pallas as pl
from jax.experimental.pallas import tpu as pltpu
from jax.sharding import PartitionSpec as P

MESH = pl.DeviceIdType.MESH
F32 = jnp.float32
BF16 = jnp.bfloat16
NT = (((1,), (1,)), ((), ()))


def split_bf16(x):
    hi = x.astype(BF16)
    return hi, (x - hi.astype(F32)).astype(BF16)


def screen_kernel(
    inj, mon, out, ids_from, ids_to, hour_ids, ratings,
    result,
    a, b32, bl, bthi, btlo, onehot, ahi, alo,
    part, parts3, tot, qsum, lod, flow, send_flow, recv_flow, packs, fscr, lscr, accs,
    zs, zr, ys, yr, cs, cr, bsem, xs, xr, fs, fr, pzs, pzr, pys, pyr, pcs, pcr,
):
    me = lax.axis_index("branch")
    bus = lax.axis_index("bus")
    width = mon.shape[1]
    mrows, orows = mon.shape[0], out.shape[0]
    z = me // 4
    y = (me // 2) % 2
    p = me % 2
    oy = 1 - y
    x = bus // 2
    h = bus % 2
    up = {"branch": (me + 4) % 32}
    down = {"branch": (me + 28) % 32}
    across = {"branch": z * 4 + oy * 2 + p}
    mate = {"branch": z * 4 + y * 2 + (1 - p)}

    load_b = [
        pltpu.make_async_copy(mon, b32.at[pl.ds(0, mrows)], bsem.at[0]),
        pltpu.make_async_copy(out, b32.at[pl.ds(mrows, orows)], bsem.at[1]),
    ]
    own_copy = [
        pltpu.make_async_copy(inj.at[pl.ds(8 * e, 8)], a.at[z, y, p, e], bsem.at[2 + e])
        for e in range(2)
    ]
    for c in load_b + own_copy:
        c.start()

    barrier = pltpu.get_barrier_semaphore()
    peers = [across, mate]
    peers += [{"branch": (me + 4 * k) % 32} for k in range(1, 8)]
    peers += [{"bus": (bus + k) % 8} for k in range(1, 8)]
    for d in peers:
        pl.semaphore_signal(barrier, inc=1, device_id=d, device_id_type=MESH)
    pl.semaphore_wait(barrier, len(peers))

    def slot(delta):
        return (z + (delta + 8)) % 8

    def chunk(delta, yy, pp, e):
        return a.at[slot(delta), yy, pp, e]

    sends = []

    def send(src, dst, ssem, rsem, dev):
        c = pltpu.make_async_remote_copy(
            src_ref=src, dst_ref=dst, send_sem=ssem, recv_sem=rsem,
            device_id=dev, device_id_type=MESH,
        )
        c.start()
        sends.append(c)

    def arrived(ref, rsem):
        pltpu.make_async_remote_copy(
            src_ref=ref, dst_ref=ref, send_sem=rsem, recv_sem=rsem,
            device_id=mate, device_id_type=MESH,
        ).wait_recv()

    def z_item(direction, item):
        if item < 6:
            return item // 2 + 1, item % 2, y
        if item == 6:
            return 4, direction, y
        return item - 6, 0, oy

    def send_z(direction, item):
        sign = 1 if direction == 0 else -1
        step, e, yy = z_item(direction, item)
        dst = chunk(-sign * (step - 1), yy, p, e)
        src = inj.at[pl.ds(8 * e, 8)] if item < 2 else dst
        send(src, dst, zs.at[direction, item], zr.at[direction, item], up if direction == 0 else down)

    def recv_z(direction, item):
        sign = 1 if direction == 0 else -1
        step, e, yy = z_item(direction, item)
        delta = -sign * step
        arrived(chunk(delta, yy, p, e), zr.at[direction, item])
        return lambda: send_c(delta, yy, e)

    y_items = [(0, 0), (0, 1), (-1, 1), (1, 1), (-2, 1), (2, 1), (-3, 1), (3, 1), (-4, 0), (-4, 1)]

    def send_y(item):
        delta, e = y_items[item]
        dst = chunk(delta, y, p, e)
        src = inj.at[pl.ds(8 * e, 8)] if item < 2 else dst
        send(src, dst, ys.at[item], yr.at[item], across)

    def recv_y(item):
        delta, e = y_items[item]
        arrived(chunk(delta, oy, p, e), yr.at[item])
        return lambda: send_c(delta, oy, e)

    c_items = []

    def send_c(delta, yy, e):
        item = len(c_items)
        other = 0 if yy is y else 1
        c_items.append((delta % 8, other, e))
        dst = chunk(delta, yy, p, e)
        src = inj.at[pl.ds(8 * e, 8)] if (delta == 0 and other == 0) else dst
        send(src, dst, cs.at[item], cr.at[item], mate)

    got_c = set()

    def recv_c(pieces):
        for delta, other, e in pieces:
            item = c_items.index((delta % 8, other, e))
            if item not in got_c:
                got_c.add(item)
                arrived(chunk(delta, oy if other else y, 1 - p, e), cr.at[item])

    tiles = width // 128

    def block(pieces):
        recv_c(pieces)
        for n, (delta, other, e) in enumerate(pieces):
            hi, lo = split_bf16(a[slot(delta), oy if other else y, :, e].reshape(16, width))
            ahi[pl.ds(16 * n, 16)] = hi
            alo[pl.ds(16 * n, 16)] = lo
        top = pl.ds(0, 16 * len(pieces))
        acc = jnp.dot(ahi[top], bthi[...], preferred_element_type=F32)
        acc = acc + jnp.dot(alo[top], bthi[...], preferred_element_type=F32)
        acc = acc + jnp.dot(ahi[top], btlo[...], preferred_element_type=F32)
        for n, (delta, other, e) in enumerate(pieces):
            for pp in range(2):
                row = pl.multiple_of(32 * (oy if other else y) + 16 * pp + 8 * e, 8)
                flow[slot(delta), pl.ds(row, 8)] = acc[16 * n + 8 * pp:16 * n + 8 * pp + 8]

    def flow_copy(delta):
        to = slot(delta)
        k = (to - bus + 8) % 8
        return k, pltpu.make_async_remote_copy(
            src_ref=send_flow.at[to], dst_ref=recv_flow.at[k],
            send_sem=fs.at[delta % 8], recv_sem=fr.at[k],
            device_id={"bus": to}, device_id_type=MESH,
        )

    def finish(deltas):
        for delta in deltas:
            k = slot(delta)
            send_flow[k, pl.ds(0, 64)] = flow[k, :, pl.ds(0, mrows)]
            tail = flow[k, :, pl.ds(mrows, orows)]
            send_flow[k, pl.ds(64, 32)] = jnp.concatenate([tail[:32], tail[32:]], axis=1)
        for delta in deltas:
            away, copy = flow_copy(delta)

            @pl.when(away != 0)
            def _():
                copy.start()

    shift = bus * width

    def transposed_b(first, last):
        def step(j, _):
            cols = pl.ds(pl.multiple_of(j * 128, 128), 128)
            for r, n in ((0, mrows), (mrows, orows)):
                hi, lo = split_bf16(b32[pl.ds(r, n), cols].T)
                bthi[cols, pl.ds(r, n)] = hi
                btlo[cols, pl.ds(r, n)] = lo
            return 0

        lax.fori_loop(first, last, step, 0)

    def left_b():
        for r in range(0, mrows, 32):
            hi, lo = split_bf16(b32[pl.ds(r, 32)])
            bl[pl.ds(r, 32)] = hi
            bl[pl.ds(mrows + r, 32)] = lo

    def index_rows(start, size):
        cols = pl.ds(pl.multiple_of(start, 128), size)
        f = ids_from[:, cols] - shift
        t = ids_to[:, cols] - shift
        same = f == t
        f = jnp.where(same | (f < 0) | (f >= width), -1, f)
        t = jnp.where(same | (t < 0) | (t >= width), -1, t)
        return f, t

    def self_part():
        chip = me // 2
        f, t = index_rows(chip * 128, 128)
        f = jnp.broadcast_to(f, (128, 128)).T
        t = jnp.broadcast_to(t, (128, 128)).T
        mine = p == 0
        f = jnp.where(mine, f[:orows], f[orows:])
        t = jnp.where(mine, t[:orows], t[orows:])
        lane = lax.broadcasted_iota(jnp.int32, (1, 128), 1)

        def step(j, acc):
            cols = pl.ds(pl.multiple_of(j * 128, 128), 128)
            v = b32[pl.ds(mrows, orows), cols]
            at = lane + j * 128
            return acc + jnp.where(f == at, v, 0.0) - jnp.where(t == at, v, 0.0)

        acc = lax.fori_loop(0, tiles, step, jnp.zeros((orows, 128), F32))
        acc = jnp.concatenate([acc, jnp.zeros((128 - orows, 128), F32)], axis=0)
        row = jnp.sum(acc.T, axis=0, keepdims=True)
        for k in range(8):
            send_flow[k, pl.ds(96, 8)] = jnp.broadcast_to(row, (8, 128))

    def sens_part(d, half):
        i = (x + d) % 4
        f, t = index_rows(i * 512 + half * 256, 256)
        f = jnp.broadcast_to(f, (128, 256)).astype(jnp.int16)
        t = jnp.broadcast_to(t, (128, 256)).astype(jnp.int16)
        sub = lax.broadcasted_iota(jnp.int32, (128, 256), 0).astype(jnp.int16)
        one, zero = jnp.ones((128, 256), BF16), jnp.zeros((128, 256), BF16)

        def step(j, _):
            at = sub + (j * 128).astype(jnp.int16)
            onehot[pl.ds(pl.multiple_of(j * 128, 128), 128)] = jnp.where(
                f == at, one, jnp.where(t == at, -one, zero)
            )
            return 0

        lax.fori_loop(0, tiles, step, 0)
        acc = jnp.dot(bl[...], onehot[...], preferred_element_type=F32)
        part[i, :, pl.ds(half * 256, 256)] = acc[:mrows] + acc[mrows:]

    def x_dev(d):
        return {"bus": ((x + d) % 4) * 2 + h}

    def send_part(d):
        send(part.at[(x + d) % 4], parts3.at[d - 1], xs.at[d - 1], xr.at[d - 1], x_dev(d))

    def sum_part():
        for d in (1, 2, 3):
            arrived(parts3.at[d - 1], xr.at[d - 1])
        tot[...] = part[x] + parts3[0] + parts3[1] + parts3[2]
        send(tot, qsum, xs.at[3], xr.at[3], {"bus": x * 2 + (1 - h)})

    def share_part():
        arrived(qsum, xr.at[3])
        sends[pair_send[0]].wait_send()
        lod[x] = tot[...] + qsum[...]
        for d in (1, 2, 3):
            send(lod.at[x], lod.at[x], xs.at[3 + d], xr.at[3 + d], x_dev(d))

    def take_part():
        for d in (1, 2, 3):
            arrived(lod.at[(x + 4 - d) % 4], xr.at[3 + d])

    pair_send = []

    def both(f, *items):
        for item in items:
            for d in (0, 1):
                f(d, item)

    def recv_both(item):
        return [recv_z(0, item), recv_z(1, item)]

    def run(fs_):
        for f_ in fs_:
            f_()

    for e in range(2):
        send_z(0, e)
        send_z(1, e)
        send_y(e)
        send_c(0, y, e)
    for c in load_b:
        c.wait()
    left_b()
    for c in own_copy:
        c.wait()
    sens_part(2, 0)
    q = recv_both(0)
    both(send_z, 2)
    run(q + [recv_y(0)])
    sens_part(2, 1)
    send_part(2)
    sens_part(1, 0)
    q = recv_both(1)
    both(send_z, 3)
    send_y(2), send_y(3)
    run(q + [recv_y(1)])
    sens_part(1, 1)
    send_part(1)
    sens_part(3, 0)
    q = recv_both(2)
    both(send_z, 4)
    run(q)
    sens_part(3, 1)
    send_part(3)
    q = recv_both(3)
    both(send_z, 5, 7)
    send_y(4), send_y(5)
    run(q + [recv_y(2), recv_y(3)])
    sens_part(0, 0)
    sens_part(0, 1)
    q = [recv_z(0, 4)]
    send_z(0, 6)
    run(q + [recv_z(1, 4)])
    sum_part()
    pair_send.append(len(sends) - 1)
    self_part()
    transposed_b(0, tiles // 2)
    q = recv_both(5)
    send_z(1, 6)
    send_y(6), send_y(7)
    run(q + [recv_y(4), recv_y(5)])
    transposed_b(tiles // 2, tiles)
    share_part()
    q = recv_both(7)
    both(send_z, 8)
    run(q)
    block([(d, o, e) for d in (0, 1, -1) for o in (0, 1) for e in (0, 1)])
    finish((0, 1, -1))
    q = [recv_z(0, 6), recv_z(1, 6)]
    send_y(8), send_y(9)
    run(q + [recv_y(6), recv_y(7)])
    block([(d, 0, e) for d in (3, -3, 4) for e in (0, 1)] + [(3, 1, 1), (-3, 1, 1)])
    q = recv_both(8)
    both(send_z, 9)
    run(q)
    block([(d, o, e) for d in (2, -2) for o in (0, 1) for e in (0, 1)])
    finish((2, -2))

    def pack_z(k):
        return pltpu.make_async_remote_copy(
            src_ref=packs.at[z, y, p], dst_ref=packs.at[z, y, p], send_sem=pzs.at[k], recv_sem=pzr.at[k],
            device_id={"branch": (me + 4 * k) % 32}, device_id_type=MESH,
        )

    def own_sum():
        own = send_flow[bus]
        for k in range(1, 8):
            arrived(recv_flow.at[k], fr.at[k])
            own = own + recv_flow[k]
        recv_flow[0] = own
        packs[z, y, p] = own[64:]
        for k in (4, 3, 5, 2, 6, 1, 7):
            pack_z(k).start()

    order = (0, 1, 7, 2, 6, 3, 5, 4)

    def forward_z():
        for k in order:
            zz = (z - k + 8) % 8
            ref = packs.at[zz, y, p]
            if k:
                arrived(ref, pzr.at[k])
            send(ref, ref, pys.at[k], pyr.at[k], across)
            send(ref, ref, pcs.at[k], pcr.at[k], mate)

    def forward_y():
        for k in order:
            ref = packs.at[(z - k + 8) % 8, oy, p]
            arrived(ref, pyr.at[k])
            send(ref, ref, pcs.at[8 + k], pcr.at[8 + k], mate)

    low = lax.broadcasted_iota(jnp.int32, (1, 128), 1) < 64

    def take_lod():
        for n, k in enumerate(order):
            zz = (z - k + 8) % 8
            for yy in range(2):
                cols = pl.ds(pl.multiple_of((zz % 2 * 2 + yy) * 128, 128), 128)
                lscr[2 * n + yy] = lod[zz // 2, :, cols]

    def take_packs():
        for n, k in enumerate(order):
            zz = (z - k + 8) % 8
            arrived(packs.at[zz, y, 1 - p], pcr.at[k])
            arrived(packs.at[zz, oy, 1 - p], pcr.at[8 + k])
            for yy in range(2):
                at = 2 * n + yy
                p0, p1 = packs[zz, yy, 0], packs[zz, yy, 1]
                r0, r1 = pltpu.roll(p0, 64, 1), pltpu.roll(p1, 64, 1)
                one = jnp.where(low, p0, r1)
                two = jnp.where(low, r0, p1)
                scale = 1.0 / jnp.maximum(1.0 - one[32:33], 0.25)
                fscr[at, pl.ds(0, 32)] = one[:32] * scale
                fscr[at, pl.ds(32, 32)] = two[:32] * scale

    lane = lax.broadcasted_iota(jnp.int32, (1, 1, 128), 2)
    hb, mt = 4, 4

    def screen(first, last, g0, g1):
        def screen_m(g, _):
            rows = pl.ds(pl.multiple_of(g * (8 * mt), 8 * mt), 8 * mt)

            def reduce_last(n, carry):
                top, bot = carry
                for i in range(hb):
                    here = lane == (n - 1) * hb + i
                    most = jnp.max(accs[0, i], axis=2, keepdims=True)
                    least = jnp.min(accs[1, i], axis=2, keepdims=True)
                    top = jnp.maximum(top, jnp.where(here, most, 0.0))
                    bot = jnp.minimum(bot, jnp.where(here, least, 0.0))
                return top, bot

            def screen_h(n, carry):
                carry = reduce_last(n, carry)
                hi = [jnp.zeros((mt, 8, 128), F32) for _ in range(hb)]
                lo = [jnp.zeros((mt, 8, 128), F32) for _ in range(hb)]
                for kb in range(first, last):
                    l = lscr[kb, rows].reshape(mt, 8, 128)
                    for i in range(hb):
                        f = fscr[kb, pl.ds(n * hb + i, 8, stride=0)]
                        v = l * f[None]
                        hi[i] = jnp.maximum(hi[i], v)
                        lo[i] = jnp.minimum(lo[i], v)
                for i in range(hb):
                    accs[0, i] = hi[i]
                    accs[1, i] = lo[i]
                return carry

            zero = jnp.zeros((mt, 8, 128), F32)
            accs[...] = jnp.zeros(accs.shape, F32)
            carry = lax.fori_loop(0, 64 // hb, screen_h, (zero, zero))
            top, bot = reduce_last(64 // hb, carry)
            parts3[0, rows, pl.ds(0, 128)] = top.reshape(8 * mt, 128)
            parts3[1, rows, pl.ds(0, 128)] = bot.reshape(8 * mt, 128)
            return 0

        lax.fori_loop(g0, g1, screen_m, 0)

    groups = mrows // (8 * mt)

    for item in (8, 9):
        recv_y(item)()
    for d in (0, 1):
        recv_z(d, 9)()
    block([(3, 1, 0), (-3, 1, 0), (4, 1, 0), (4, 1, 1)])
    finish((3, -3, 4))
    own_sum()
    take_part()
    take_lod()
    forward_z()
    forward_y()
    take_packs()
    screen(0, 16, 0, groups)
    base = recv_flow[0, pl.ds(0, 64)]
    worst = jnp.maximum(
        jnp.abs(base + parts3[0, :, pl.ds(0, 128)].T[:64]), jnp.abs(base + parts3[1, :, pl.ds(0, 128)].T[:64])
    )
    hour = jnp.concatenate([hour_ids[...], jnp.zeros((1, 64), jnp.int32)], axis=1)
    season = ((jnp.broadcast_to(hour, (128, 128)).T)[:64] * 4) // 8760
    rating = jnp.where(season == 0, ratings[0:1], ratings[1:2])
    rating = jnp.where(season == 2, ratings[2:3], rating)
    rating = jnp.where(season == 3, ratings[3:4], rating)
    result[...] = worst / rating
    for k in range(1, 8):
        pack_z(k).wait_send()
    for delta in range(8):
        away, copy = flow_copy(delta)

        @pl.when(away != 0)
        def _():
            copy.wait_send()

    done = set(pair_send)
    for n, c in enumerate(sends):
        if n not in done:
            c.wait_send()


def on_device(injections, ptdf_mon, ptdf_out, outage_from, outage_to, hour_ids, ratings):
    mrows, width = ptdf_mon.shape
    orows = ptdf_out.shape[0]
    rows = mrows + orows
    hbm = pl.BlockSpec(memory_space=pl.ANY)
    vmem = pl.BlockSpec(memory_space=pltpu.VMEM)
    dma = pltpu.SemaphoreType.DMA
    v = pltpu.VMEM
    return pl.pallas_call(
        screen_kernel,
        out_shape=jax.ShapeDtypeStruct((64, mrows), F32),
        in_specs=[hbm, hbm, hbm, vmem, vmem, vmem, vmem],
        out_specs=vmem,
        scratch_shapes=[
            v((8, 2, 2, 2, 8, width), F32),
            v((rows, width), F32),
            v((2 * mrows, width), BF16),
            v((width, rows), BF16),
            v((width, rows), BF16),
            v((width, 256), BF16),
            v((192, width), BF16),
            v((192, width), BF16),
            v((4, mrows, 512), F32),
            v((3, mrows, 512), F32),
            v((mrows, 512), F32),
            v((mrows, 512), F32),
            v((4, mrows, 512), F32),
            v((8, 64, rows), F32),
            v((8, 104, 128), F32),
            v((8, 104, 128), F32),
            v((8, 2, 2, 40, 128), F32),
            v((16, 64, 128), F32),
            v((16, mrows, 128), F32),
            v((2, 4, 4, 8, 128), F32),
            dma((2, 10)), dma((2, 10)), dma((10,)), dma((10,)), dma((32,)), dma((32,)), dma((4,)),
            dma((7,)), dma((7,)), dma((8,)), dma((8,)), dma((8,)), dma((8,)), dma((8,)), dma((8,)),
            dma((16,)), dma((16,)),
        ],
        compiler_params=pltpu.CompilerParams(
            collective_id=0, has_side_effects=True, vmem_limit_bytes=64 * 1024 * 1024 - 128 * 1024
        ),
        name="screen",
    )(
        injections, ptdf_mon, ptdf_out, outage_from.reshape(1, -1), outage_to.reshape(1, -1),
        hour_ids.reshape(1, -1), ratings.T,
    )


def solution(mesh):
    placed = (
        P("branch", "bus"),
        P("branch", "bus"),
        P("branch", "bus"),
        P(),
        P(),
        P("bus"),
        P("branch", None),
    )
    return jax.shard_map(
        on_device, mesh=mesh, in_specs=placed, out_specs=P("bus", "branch"), check_vma=False
    )
```

```python
import functools

import jax
import jax.numpy as jnp
from jax import lax
from jax.experimental import pallas as pl
from jax.experimental.pallas import tpu as pltpu
from jax.sharding import PartitionSpec as P

MESH = pl.DeviceIdType.MESH
F32 = jnp.float32
BF16 = jnp.bfloat16
NT = (((1,), (1,)), ((), ()))


def split_bf16(x):
    hi = x.astype(BF16)
    return hi, (x - hi.astype(F32)).astype(BF16)


def screen_kernel(
    inj, mon, out, ids_from, ids_to, hour_ids, ratings,
    result,
    a, b32, bl, bthi, btlo, onehot, ahi, alo,
    part, parts3, tot, qsum, lod, flow, send_flow, recv_flow, packs, fscr, lscr, accs,
    zs, zr, ys, yr, cs, cr, bsem, xs, xr, fs, fr, pzs, pzr, pys, pyr, pcs, pcr,
):
    me = lax.axis_index("branch")
    bus = lax.axis_index("bus")
    width = mon.shape[1]
    mrows, orows = mon.shape[0], out.shape[0]
    z = me // 4
    y = (me // 2) % 2
    p = me % 2
    oy = 1 - y
    x = bus // 2
    h = bus % 2
    up = {"branch": (me + 4) % 32}
    down = {"branch": (me + 28) % 32}
    across = {"branch": z * 4 + oy * 2 + p}
    mate = {"branch": z * 4 + y * 2 + (1 - p)}

    load_b = [
        pltpu.make_async_copy(mon, b32.at[pl.ds(0, mrows)], bsem.at[0]),
        pltpu.make_async_copy(out, b32.at[pl.ds(mrows, orows)], bsem.at[1]),
    ]
    own_copy = [
        pltpu.make_async_copy(inj.at[pl.ds(8 * e, 8)], a.at[z, y, p, e], bsem.at[2 + e])
        for e in range(2)
    ]
    for c in load_b + own_copy:
        c.start()

    barrier = pltpu.get_barrier_semaphore()
    peers = [across, mate]
    peers += [{"branch": (me + 4 * k) % 32} for k in range(1, 8)]
    peers += [{"bus": (bus + k) % 8} for k in range(1, 8)]
    for d in peers:
        pl.semaphore_signal(barrier, inc=1, device_id=d, device_id_type=MESH)
    pl.semaphore_wait(barrier, len(peers))

    def slot(delta):
        return (z + (delta + 8)) % 8

    def chunk(delta, yy, pp, e):
        return a.at[slot(delta), yy, pp, e]

    sends = []

    def send(src, dst, ssem, rsem, dev):
        c = pltpu.make_async_remote_copy(
            src_ref=src, dst_ref=dst, send_sem=ssem, recv_sem=rsem,
            device_id=dev, device_id_type=MESH,
        )
        c.start()
        sends.append(c)

    def arrived(ref, rsem):
        pltpu.make_async_remote_copy(
            src_ref=ref, dst_ref=ref, send_sem=rsem, recv_sem=rsem,
            device_id=mate, device_id_type=MESH,
        ).wait_recv()

    def z_item(direction, item):
        if item < 6:
            return item // 2 + 1, item % 2, y
        if item == 6:
            return 4, direction, y
        return item - 6, 0, oy

    def send_z(direction, item):
        sign = 1 if direction == 0 else -1
        step, e, yy = z_item(direction, item)
        dst = chunk(-sign * (step - 1), yy, p, e)
        src = inj.at[pl.ds(8 * e, 8)] if item < 2 else dst
        send(src, dst, zs.at[direction, item], zr.at[direction, item], up if direction == 0 else down)

    def recv_z(direction, item):
        sign = 1 if direction == 0 else -1
        step, e, yy = z_item(direction, item)
        delta = -sign * step
        arrived(chunk(delta, yy, p, e), zr.at[direction, item])
        return lambda: send_c(delta, yy, e)

    y_items = [(0, 0), (0, 1), (-1, 1), (1, 1), (-2, 1), (2, 1), (-3, 1), (3, 1), (-4, 0), (-4, 1)]

    def send_y(item):
        delta, e = y_items[item]
        dst = chunk(delta, y, p, e)
        src = inj.at[pl.ds(8 * e, 8)] if item < 2 else dst
        send(src, dst, ys.at[item], yr.at[item], across)

    def recv_y(item):
        delta, e = y_items[item]
        arrived(chunk(delta, oy, p, e), yr.at[item])
        return lambda: send_c(delta, oy, e)

    c_items = []

    def send_c(delta, yy, e):
        item = len(c_items)
        other = 0 if yy is y else 1
        c_items.append((delta % 8, other, e))
        dst = chunk(delta, yy, p, e)
        src = inj.at[pl.ds(8 * e, 8)] if (delta == 0 and other == 0) else dst
        send(src, dst, cs.at[item], cr.at[item], mate)

    got_c = set()

    def recv_c(pieces):
        for delta, other, e in pieces:
            item = c_items.index((delta % 8, other, e))
            if item not in got_c:
                got_c.add(item)
                arrived(chunk(delta, oy if other else y, 1 - p, e), cr.at[item])

    tiles = width // 128

    def block(pieces):
        recv_c(pieces)
        for n, (delta, other, e) in enumerate(pieces):
            hi, lo = split_bf16(a[slot(delta), oy if other else y, :, e].reshape(16, width))
            ahi[pl.ds(16 * n, 16)] = hi
            alo[pl.ds(16 * n, 16)] = lo
        top = pl.ds(0, 16 * len(pieces))
        acc = jnp.dot(ahi[top], bthi[...], preferred_element_type=F32)
        acc = acc + jnp.dot(alo[top], bthi[...], preferred_element_type=F32)
        acc = acc + jnp.dot(ahi[top], btlo[...], preferred_element_type=F32)
        for n, (delta, other, e) in enumerate(pieces):
            for pp in range(2):
                row = pl.multiple_of(32 * (oy if other else y) + 16 * pp + 8 * e, 8)
                flow[slot(delta), pl.ds(row, 8)] = acc[16 * n + 8 * pp:16 * n + 8 * pp + 8]

    def flow_copy(delta):
        to = slot(delta)
        k = (to - bus + 8) % 8
        return k, pltpu.make_async_remote_copy(
            src_ref=send_flow.at[to], dst_ref=recv_flow.at[k],
            send_sem=fs.at[delta % 8], recv_sem=fr.at[k],
            device_id={"bus": to}, device_id_type=MESH,
        )

    def finish(deltas):
        for delta in deltas:
            k = slot(delta)
            send_flow[k, pl.ds(0, 64)] = flow[k, :, pl.ds(0, mrows)]
            tail = flow[k, :, pl.ds(mrows, orows)]
            send_flow[k, pl.ds(64, 32)] = jnp.concatenate([tail[:32], tail[32:]], axis=1)
        for delta in deltas:
            away, copy = flow_copy(delta)

            @pl.when(away != 0)
            def _():
                copy.start()

    shift = bus * width

    def transposed_b(first, last):
        def step(j, _):
            cols = pl.ds(pl.multiple_of(j * 128, 128), 128)
            for r, n in ((0, mrows), (mrows, orows)):
                hi, lo = split_bf16(b32[pl.ds(r, n), cols].T)
                bthi[cols, pl.ds(r, n)] = hi
                btlo[cols, pl.ds(r, n)] = lo
            return 0

        lax.fori_loop(first, last, step, 0)

    def left_b():
        for r in range(0, mrows, 32):
            hi, lo = split_bf16(b32[pl.ds(r, 32)])
            bl[pl.ds(r, 32)] = hi
            bl[pl.ds(mrows + r, 32)] = lo

    def index_rows(start, size):
        cols = pl.ds(pl.multiple_of(start, 128), size)
        f = ids_from[:, cols] - shift
        t = ids_to[:, cols] - shift
        same = f == t
        f = jnp.where(same | (f < 0) | (f >= width), -1, f)
        t = jnp.where(same | (t < 0) | (t >= width), -1, t)
        return f, t

    def self_part():
        chip = me // 2
        f, t = index_rows(chip * 128, 128)
        f = jnp.broadcast_to(f, (128, 128)).T
        t = jnp.broadcast_to(t, (128, 128)).T
        mine = p == 0
        f = jnp.where(mine, f[:orows], f[orows:])
        t = jnp.where(mine, t[:orows], t[orows:])
        lane = lax.broadcasted_iota(jnp.int32, (1, 128), 1)

        def step(j, acc):
            cols = pl.ds(pl.multiple_of(j * 128, 128), 128)
            v = b32[pl.ds(mrows, orows), cols]
            at = lane + j * 128
            return acc + jnp.where(f == at, v, 0.0) - jnp.where(t == at, v, 0.0)

        acc = lax.fori_loop(0, tiles, step, jnp.zeros((orows, 128), F32))
        acc = jnp.concatenate([acc, jnp.zeros((128 - orows, 128), F32)], axis=0)
        row = jnp.sum(acc.T, axis=0, keepdims=True)
        for k in range(8):
            send_flow[k, pl.ds(96, 8)] = jnp.broadcast_to(row, (8, 128))

    def sens_part(d, half):
        i = (x + d) % 4
        f, t = index_rows(i * 512 + half * 256, 256)
        f = jnp.broadcast_to(f, (128, 256)).astype(jnp.int16)
        t = jnp.broadcast_to(t, (128, 256)).astype(jnp.int16)
        sub = lax.broadcasted_iota(jnp.int32, (128, 256), 0).astype(jnp.int16)
        one, zero = jnp.ones((128, 256), BF16), jnp.zeros((128, 256), BF16)

        def step(j, _):
            at = sub + (j * 128).astype(jnp.int16)
            onehot[pl.ds(pl.multiple_of(j * 128, 128), 128)] = jnp.where(
                f == at, one, jnp.where(t == at, -one, zero)
            )
            return 0

        lax.fori_loop(0, tiles, step, 0)
        acc = jnp.dot(bl[...], onehot[...], preferred_element_type=F32)
        part[i, :, pl.ds(half * 256, 256)] = acc[:mrows] + acc[mrows:]

    def x_dev(d):
        return {"bus": ((x + d) % 4) * 2 + h}

    def send_part(d):
        send(part.at[(x + d) % 4], parts3.at[d - 1], xs.at[d - 1], xr.at[d - 1], x_dev(d))

    def sum_part():
        for d in (1, 2, 3):
            arrived(parts3.at[d - 1], xr.at[d - 1])
        tot[...] = part[x] + parts3[0] + parts3[1] + parts3[2]
        send(tot, qsum, xs.at[3], xr.at[3], {"bus": x * 2 + (1 - h)})

    def share_part():
        arrived(qsum, xr.at[3])
        sends[pair_send[0]].wait_send()
        lod[x] = tot[...] + qsum[...]
        for d in (1, 2, 3):
            send(lod.at[x], lod.at[x], xs.at[3 + d], xr.at[3 + d], x_dev(d))

    def take_part():
        for d in (1, 2, 3):
            arrived(lod.at[(x + 4 - d) % 4], xr.at[3 + d])

    pair_send = []

    def both(f, *items):
        for item in items:
            for d in (0, 1):
                f(d, item)

    def recv_both(item):
        return [recv_z(0, item), recv_z(1, item)]

    def run(fs_):
        for f_ in fs_:
            f_()

    for e in range(2):
        send_z(0, e)
        send_z(1, e)
        send_y(e)
        send_c(0, y, e)
    for c in load_b:
        c.wait()
    left_b()
    for c in own_copy:
        c.wait()
    sens_part(2, 0)
    q = recv_both(0)
    both(send_z, 2)
    run(q + [recv_y(0)])
    sens_part(2, 1)
    send_part(2)
    sens_part(1, 0)
    q = recv_both(1)
    both(send_z, 3)
    send_y(2), send_y(3)
    run(q + [recv_y(1)])
    sens_part(1, 1)
    send_part(1)
    sens_part(3, 0)
    q = recv_both(2)
    both(send_z, 4)
    run(q)
    sens_part(3, 1)
    send_part(3)
    q = recv_both(3)
    both(send_z, 5, 7)
    send_y(4), send_y(5)
    run(q + [recv_y(2), recv_y(3)])
    sens_part(0, 0)
    sens_part(0, 1)
    q = [recv_z(0, 4)]
    send_z(0, 6)
    run(q + [recv_z(1, 4)])
    sum_part()
    pair_send.append(len(sends) - 1)
    self_part()
    transposed_b(0, tiles // 2)
    q = recv_both(5)
    send_z(1, 6)
    send_y(6), send_y(7)
    run(q + [recv_y(4), recv_y(5)])
    transposed_b(tiles // 2, tiles)
    share_part()
    q = recv_both(7)
    both(send_z, 8)
    run(q)
    block([(d, o, e) for d in (0, 1, -1) for o in (0, 1) for e in (0, 1)])
    finish((0, 1, -1))
    q = [recv_z(0, 6), recv_z(1, 6)]
    send_y(8), send_y(9)
    run(q + [recv_y(6), recv_y(7)])
    block([(d, 0, e) for d in (3, -3, 4) for e in (0, 1)] + [(3, 1, 1), (-3, 1, 1)])
    q = recv_both(8)
    both(send_z, 9)
    run(q)
    near, middle, far = (0, 1, -1), (2, -2), (3, -3, 4)
    is_near = (bus - z + 9) % 8 < 3

    def pack_z(k):
        return pltpu.make_async_remote_copy(
            src_ref=packs.at[z, y, p], dst_ref=packs.at[z, y, p], send_sem=pzs.at[k], recv_sem=pzr.at[k],
            device_id={"branch": (me + 4 * k) % 32}, device_id_type=MESH,
        )

    def own_sum():
        own = send_flow[bus]
        for k in range(1, 8):
            arrived(recv_flow.at[k], fr.at[k])
            own = own + recv_flow[k]
        recv_flow[0] = own
        packs[z, y, p] = own[64:]
        for k in (4, 3, 5, 2, 6, 1, 7):
            pack_z(k).start()

    def forward_z(which):
        for d in which:
            zz = (bus + d + 8) % 8
            k = (z - zz + 8) % 8

            @pl.when(k != 0)
            def _():
                arrived(packs.at[zz, y, p], pzr.at[k])

            send(packs.at[zz, y, p], packs.at[zz, y, p], pys.at[d % 8], pyr.at[d % 8], across)
            send(packs.at[zz, y, p], packs.at[zz, y, p], pcs.at[d % 8], pcr.at[d % 8], mate)

    def forward_y(which):
        for d in which:
            zz = (bus + d + 8) % 8
            arrived(packs.at[zz, oy, p], pyr.at[d % 8])
            send(packs.at[zz, oy, p], packs.at[zz, oy, p], pcs.at[8 + d % 8], pcr.at[8 + d % 8], mate)

    low = lax.broadcasted_iota(jnp.int32, (1, 128), 1) < 64

    def take_packs(which, first):
        for n, d in enumerate(which):
            zz = (bus + d + 8) % 8
            arrived(packs.at[zz, y, 1 - p], pcr.at[d % 8])
            arrived(packs.at[zz, oy, 1 - p], pcr.at[8 + d % 8])
            for yy in range(2):
                at = first + 2 * n + yy
                p0, p1 = packs[zz, yy, 0], packs[zz, yy, 1]
                r0, r1 = pltpu.roll(p0, 64, 1), pltpu.roll(p1, 64, 1)
                one = jnp.where(low, p0, r1)
                two = jnp.where(low, r0, p1)
                scale = 1.0 / jnp.maximum(1.0 - one[32:33], 0.25)
                fscr[at, pl.ds(0, 32)] = one[:32] * scale
                fscr[at, pl.ds(32, 32)] = two[:32] * scale
                cols = pl.ds(pl.multiple_of((zz % 2 * 2 + yy) * 128, 128), 128)
                lscr[at] = lod[zz // 2, :, cols]

    lane = lax.broadcasted_iota(jnp.int32, (1, 1, 128), 2)
    hb, mt = 4, 4

    def screen(first, last, g0, g1):
        def screen_m(g, _):
            rows = pl.ds(pl.multiple_of(g * (8 * mt), 8 * mt), 8 * mt)

            def reduce_last(n, carry):
                top, bot = carry
                for i in range(hb):
                    here = lane == (n - 1) * hb + i
                    most = jnp.max(accs[0, i], axis=2, keepdims=True)
                    least = jnp.min(accs[1, i], axis=2, keepdims=True)
                    top = jnp.maximum(top, jnp.where(here, most, 0.0))
                    bot = jnp.minimum(bot, jnp.where(here, least, 0.0))
                return top, bot

            def screen_h(n, carry):
                carry = reduce_last(n, carry)
                hi = [jnp.zeros((mt, 8, 128), F32) for _ in range(hb)]
                lo = [jnp.zeros((mt, 8, 128), F32) for _ in range(hb)]
                for kb in range(first, last):
                    l = lscr[kb, rows].reshape(mt, 8, 128)
                    for i in range(hb):
                        f = fscr[kb, pl.ds(n * hb + i, 8, stride=0)]
                        v = l * f[None]
                        hi[i] = jnp.maximum(hi[i], v)
                        lo[i] = jnp.minimum(lo[i], v)
                for i in range(hb):
                    accs[0, i] = hi[i]
                    accs[1, i] = lo[i]
                return carry

            if first == 0:
                start = (jnp.zeros((mt, 8, 128), F32), jnp.zeros((mt, 8, 128), F32))
            else:
                start = tuple(parts3[i, rows, pl.ds(0, 128)].reshape(mt, 8, 128) for i in range(2))
            accs[...] = jnp.zeros(accs.shape, F32)
            carry = lax.fori_loop(0, 64 // hb, screen_h, start)
            top, bot = reduce_last(64 // hb, carry)
            parts3[0, rows, pl.ds(0, 128)] = top.reshape(8 * mt, 128)
            parts3[1, rows, pl.ds(0, 128)] = bot.reshape(8 * mt, 128)
            return 0

        lax.fori_loop(g0, g1, screen_m, 0)

    groups = mrows // (8 * mt)

    @pl.when(is_near)
    def _():
        own_sum()

    block([(d, o, e) for d in (2, -2) for o in (0, 1) for e in (0, 1)])
    finish((2, -2))
    for item in (8, 9):
        recv_y(item)()
    for d in (0, 1):
        recv_z(d, 9)()
    block([(3, 1, 0), (-3, 1, 0), (4, 1, 0), (4, 1, 1)])
    finish((3, -3, 4))
    forward_z(near)
    take_part()
    forward_y(near)
    take_packs(near, 0)

    @pl.when(jnp.logical_not(is_near))
    def _():
        own_sum()

    screen(0, 6, 0, groups)
    forward_z(middle)
    forward_z(far)
    forward_y(middle)
    forward_y(far)
    take_packs(middle, 6)
    take_packs(far, 10)
    screen(6, 16, 0, groups)
    base = recv_flow[0, pl.ds(0, 64)]
    worst = jnp.maximum(
        jnp.abs(base + parts3[0, :, pl.ds(0, 128)].T[:64]), jnp.abs(base + parts3[1, :, pl.ds(0, 128)].T[:64])
    )
    hour = jnp.concatenate([hour_ids[...], jnp.zeros((1, 64), jnp.int32)], axis=1)
    season = ((jnp.broadcast_to(hour, (128, 128)).T)[:64] * 4) // 8760
    rating = jnp.where(season == 0, ratings[0:1], ratings[1:2])
    rating = jnp.where(season == 2, ratings[2:3], rating)
    rating = jnp.where(season == 3, ratings[3:4], rating)
    result[...] = worst / rating
    for k in range(1, 8):
        pack_z(k).wait_send()
    for delta in range(8):
        away, copy = flow_copy(delta)

        @pl.when(away != 0)
        def _():
            copy.wait_send()

    done = set(pair_send)
    for n, c in enumerate(sends):
        if n not in done:
            c.wait_send()


def on_device(injections, ptdf_mon, ptdf_out, outage_from, outage_to, hour_ids, ratings):
    mrows, width = ptdf_mon.shape
    orows = ptdf_out.shape[0]
    rows = mrows + orows
    hbm = pl.BlockSpec(memory_space=pl.ANY)
    vmem = pl.BlockSpec(memory_space=pltpu.VMEM)
    dma = pltpu.SemaphoreType.DMA
    v = pltpu.VMEM
    return pl.pallas_call(
        screen_kernel,
        out_shape=jax.ShapeDtypeStruct((64, mrows), F32),
        in_specs=[hbm, hbm, hbm, vmem, vmem, vmem, vmem],
        out_specs=vmem,
        scratch_shapes=[
            v((8, 2, 2, 2, 8, width), F32),
            v((rows, width), F32),
            v((2 * mrows, width), BF16),
            v((width, rows), BF16),
            v((width, rows), BF16),
            v((width, 256), BF16),
            v((192, width), BF16),
            v((192, width), BF16),
            v((4, mrows, 512), F32),
            v((3, mrows, 512), F32),
            v((mrows, 512), F32),
            v((mrows, 512), F32),
            v((4, mrows, 512), F32),
            v((8, 64, rows), F32),
            v((8, 104, 128), F32),
            v((8, 104, 128), F32),
            v((8, 2, 2, 40, 128), F32),
            v((16, 64, 128), F32),
            v((16, mrows, 128), F32),
            v((2, 4, 4, 8, 128), F32),
            dma((2, 10)), dma((2, 10)), dma((10,)), dma((10,)), dma((32,)), dma((32,)), dma((4,)),
            dma((7,)), dma((7,)), dma((8,)), dma((8,)), dma((8,)), dma((8,)), dma((8,)), dma((8,)),
            dma((16,)), dma((16,)),
        ],
        compiler_params=pltpu.CompilerParams(
            collective_id=0, has_side_effects=True, vmem_limit_bytes=64 * 1024 * 1024 - 128 * 1024
        ),
        name="screen",
    )(
        injections, ptdf_mon, ptdf_out, outage_from.reshape(1, -1), outage_to.reshape(1, -1),
        hour_ids.reshape(1, -1), ratings.T,
    )


def solution(mesh):
    placed = (
        P("branch", "bus"),
        P("branch", "bus"),
        P("branch", "bus"),
        P(),
        P(),
        P("bus"),
        P("branch", None),
    )
    return jax.shard_map(
        on_device, mesh=mesh, in_specs=placed, out_specs=P("bus", "branch"), check_vma=False
    )
```
